32 devices in a mesh: groups: 2 (over y), patch: 4 (over z), sub: 2 (over x), half: 2 (over core).
Axes of the slice: x: 2, y: 2, z: 4, core: 2. Of those that a mesh axis runs over, the one named last changes fastest.
Arguments:
- vectors: float32 [2, 8192, 256], P(None, ('groups', 'patch', 'sub', 'half')), parts along dimension 1, may hold values from -600 to 600
- prestress: bfloat16 [8192, 3, 256], P(('groups', 'patch', 'sub', 'half')), parts along dimension 0, may hold values from -4 to 4
- thickness: float32 [8192, 256], P(('groups', 'patch', 'sub', 'half')), parts along dimension 0, may hold values from 0.5 to 2
- foundation: float32 [8192, 256], P(('groups', 'patch', 'sub', 'half')), parts along dimension 0, may hold values from 2 to 6
- patch_rows: int32 [64], P(('groups', 'patch', 'sub', 'half')), parts along dimension 0, may hold values from 64 to 128, as said below
- matched: int32 [64], P(('groups', 'patch', 'sub', 'half')), parts along dimension 0, may hold values from 0 to 31, as said below
- elem_row: int32 [8192], P(('groups', 'patch', 'sub', 'half')), parts along dimension 0, may hold values from 0 to 4095, as said below
Outputs:
- modes: float32 [2, 8192, 256], P(None, ('groups', 'patch', 'sub', 'half')), parts along dimension 1
The draws below stay inside these ranges and needn't reach their ends.
There are 2 independent parts, one for each index of `groups`. The reference program is written for one: setup_inputs(seed, part) draws one part's arguments, and reference() takes and returns one part's arrays. A program takes and returns all parts, laid end to end along the dimension named above; each array names one. Nothing has to cross between parts.
Inputs may be any that keep to these rules, and one draw needn't show every extreme that they name: `patch_rows`: the largest value is reached by some patch in every draw. A permutation of the patches; the patch matched to a patch lies on the device with the same sub and half indices and a patch index one above or one below, cyclically. `elem_row`: a permutation of the rows; of each device's rows, those in positions k * 16 to (k + 1) * 16 - 1 belong to patches of the device with index k along patch+sub+half.
All inputs are finite; a program needn't handle non-finite values.
Results may differ from the reference program's by a relative error of at most 0.0003.
Values may be sent and summed in bfloat16 or wider, within the bound.
A program may use at most 64 MiB of HBM per device.

```python
import math
import jax
import jax.numpy as jnp

PROWS = 128
C = 256
PSLOT = 2
ITERS = 2
PATCHES = 32
ROWS = 4096
N_PATCH = 4
N_SUB = 2
N_HALF = 2


def draw_vectors(key, part):
    first, second, third = jax.random.split(key, 3)
    row_scale = jnp.exp(jax.random.uniform(second, (2, ROWS, 1), jnp.float32, 0.0, math.log(10.0)))
    col_scale = jnp.exp(jax.random.uniform(third, (2, 1, C), jnp.float32, 0.0, math.log(10.0)))
    base = jnp.clip(jax.random.normal(first, (2, ROWS, C), jnp.float32), -6.0, 6.0)
    return base * row_scale * col_scale


def draw_patch_rows(key, part):
    first, second = jax.random.split(key)
    lengths = jax.random.randint(first, (PATCHES,), PROWS // 2, PROWS + 1).astype(jnp.int32)
    where_full = jax.random.randint(second, (), 0, PATCHES)
    return lengths.at[where_full].set(PROWS)


def draw_matched(key, part):
    groups_inner = N_SUB * N_HALF
    first, second = jax.random.split(key)
    direction = jax.random.randint(first, (groups_inner,), 0, 2).astype(jnp.int32) * 2 - 1
    direction = direction.at[0].set(1).at[1].set(-1)
    scores = jax.random.randint(second, (N_PATCH, groups_inner, PSLOT), 0, 2 ** 18).astype(jnp.int32) * PSLOT + jnp.arange(PSLOT, dtype=jnp.int32)
    slot_order = jnp.argsort(scores, axis=-1, stable=True).astype(jnp.int32)
    owner = jnp.arange(N_PATCH, dtype=jnp.int32)[:, None, None]
    inner = jnp.arange(groups_inner, dtype=jnp.int32)[None, :, None]
    target = (owner + direction[None, :, None]) % N_PATCH
    return ((target * groups_inner + inner) * PSLOT + slot_order).reshape(-1).astype(jnp.int32)


def draw_elem_row(key, part):
    devices_all = N_PATCH * N_SUB * N_HALF
    rows_dev = PSLOT * PROWS
    per_peer = rows_dev // devices_all
    scores = jax.random.randint(key, (devices_all, rows_dev), 0, 2 ** 18).astype(jnp.int32) * rows_dev + jnp.arange(rows_dev, dtype=jnp.int32)
    order = jnp.argsort(scores, axis=-1, stable=True).astype(jnp.int32)
    order = order.reshape(devices_all, devices_all, per_peer).transpose(1, 0, 2)
    owner = jnp.arange(devices_all, dtype=jnp.int32)[None, :, None]
    return (owner * rows_dev + order).reshape(-1).astype(jnp.int32)


def level_of(stream_key, extent, pieces, smallest, high):
    def one(axis_at, shards_of):
        steps = jax.random.uniform(jax.random.fold_in(jax.random.fold_in(stream_key, 6), axis_at), (shards_of,), jnp.float32, smallest / len(pieces), high / len(pieces))
        return jnp.repeat(jnp.exp(steps), extent[axis_at] // shards_of).reshape((-1,) + (1,) * (len(extent) - axis_at - 1))

    level = one(*pieces[0])
    for cut in pieces[1:]:
        level = level * one(*cut)
    return level


def noise(key, dims, scale, bound, cuts=(), held_as=jnp.bfloat16):
    level = level_of(key, dims, cuts, -0.22, 0.18) if cuts else 1.0
    result = jax.random.normal(key, dims, jnp.float32) * scale * level
    return jnp.minimum(jnp.maximum(result, -bound), bound).astype(held_as)


def setup_inputs(seed: int = 0, part: int = 0) -> dict:
    key_of = jax.random.split(jax.random.key(seed), 8)
    part_splits = jax.random.split(jax.random.fold_in(key_of[7], part), 8)
    vectors = draw_vectors(jax.random.fold_in(jax.random.fold_in(key_of[7], part), 71), part)
    prestress = noise(part_splits[1], (ROWS, 3, C), 1.0, 4.0, ((0, 16),))
    thickness = jnp.clip(jnp.exp(math.log(2.0) - 1.3862944 * jax.random.uniform(part_splits[2], (ROWS, C), jnp.float32) ** level_of(part_splits[2], (ROWS, C), ((0, 16),), -0.2, 0.2)), 0.5, 2.0)
    foundation = jnp.clip(jnp.exp(math.log(6.0) - 1.0986123 * jax.random.uniform(part_splits[3], (ROWS, C), jnp.float32) ** level_of(part_splits[3], (ROWS, C), ((0, 16),), -0.2, 0.2)), 2.0, 6.0)
    patch_rows = draw_patch_rows(jax.random.fold_in(jax.random.fold_in(key_of[7], part), 71), part)
    matched = draw_matched(jax.random.fold_in(jax.random.fold_in(key_of[7], part), 71), part)
    elem_row = draw_elem_row(jax.random.fold_in(jax.random.fold_in(key_of[7], part), 71), part)
    return {"vectors": vectors, "prestress": prestress, "thickness": thickness, "foundation": foundation, "patch_rows": patch_rows, "matched": matched, "elem_row": elem_row}


step_size = 1.0
norm_scale = 16.0
penalty_value = 8.0
penalty_slope = 4.0

def second_rows(field):
    padded = jnp.pad(field, [(0, 0)] * (field.ndim - 2) + [(1, 1), (0, 0)])
    return padded[..., :-2, :] - 2.0 * field + padded[..., 2:, :]

def second_cols(field):
    padded = jnp.pad(field, [(0, 0)] * (field.ndim - 1) + [(1, 1)])
    return padded[..., :-2] - 2.0 * field + padded[..., 2:]

def forward_rows(field):
    zeros = jnp.zeros_like(field[..., :1, :])
    return jnp.concatenate([field[..., 1:, :], zeros], axis=-2) - field

def backward_rows(field):
    zeros = jnp.zeros_like(field[..., :1, :])
    return jnp.concatenate([zeros, field[..., :-1, :]], axis=-2) - field

def forward_cols(field):
    zeros = jnp.zeros_like(field[..., :1])
    return jnp.concatenate([field[..., 1:], zeros], axis=-1) - field

def backward_cols(field):
    zeros = jnp.zeros_like(field[..., :1])
    return jnp.concatenate([zeros, field[..., :-1]], axis=-1) - field

def stiffness(field, live, thickness, foundation):
    bend_rows = thickness * live * second_rows(field)
    bend_cols = thickness * second_cols(field)
    return live * (foundation * field + second_rows(bend_rows) + second_cols(bend_cols))

def geometric(field, live, stress):
    along_rows = forward_rows(field)
    along_cols = forward_cols(field)
    nuu = stress[:, :, 0, :]
    nvv = stress[:, :, 1, :]
    nuv = stress[:, :, 2, :]
    total = backward_rows(nuu * along_rows + nuv * along_cols) + backward_cols(nvv * along_cols + nuv * along_rows)
    return live * total

def edges(field, lengths):

    def row_pick(index):
        where_rows = jnp.broadcast_to(index[None, :, None, None], (field.shape[0], field.shape[1], 1, field.shape[3]))
        return jnp.take_along_axis(field, where_rows, axis=2)[:, :, 0, :]
    top = jnp.stack([row_pick(lengths - 2), row_pick(lengths - 1)], axis=2)
    bottom = field[:, :, 0:2, :]
    return (top, bottom)

def interface(field, lengths, top, bottom, partner_top, partner_bottom):
    jump_top = top[:, :, 1, :] - partner_bottom[:, :, 0, :]
    slope_top = top[:, :, 1, :] - top[:, :, 0, :] - (partner_bottom[:, :, 1, :] - partner_bottom[:, :, 0, :])
    jump_bottom = partner_top[:, :, 1, :] - bottom[:, :, 0, :]
    slope_bottom = partner_top[:, :, 1, :] - partner_top[:, :, 0, :] - (bottom[:, :, 1, :] - bottom[:, :, 0, :])
    rows = jnp.arange(field.shape[2], dtype=jnp.int32)[None, :, None]
    last = lengths[:, None, None] - 1
    added = jnp.where(rows == last, (penalty_value * jump_top + penalty_slope * slope_top)[:, :, None, :], 0.0)
    added = added + jnp.where(rows == last - 1, (-penalty_slope * slope_top)[:, :, None, :], 0.0)
    added = added + jnp.where(rows == 0, (-penalty_value * jump_bottom + penalty_slope * slope_bottom)[:, :, None, :], 0.0)
    added = added + jnp.where(rows == 1, (-penalty_slope * slope_bottom)[:, :, None, :], 0.0)
    return added

def products(field, kfield, gfield):
    return jnp.stack([jnp.sum(field[0] * kfield[0]), jnp.sum(field[0] * kfield[1]), jnp.sum(field[1] * kfield[1]), jnp.sum(field[0] * gfield[0]), jnp.sum(field[0] * gfield[1]), jnp.sum(field[1] * gfield[1])])

def advance(field, kfield, gfield, totals, precond, cells):
    first_a = totals[0]
    cross_k = totals[1]
    second_a = totals[2]
    first_g = totals[3]
    cross_g = totals[4]
    second_g = totals[5]
    ratio = cross_k / first_a
    other = field[1] - ratio * field[0]
    other_k = kfield[1] - ratio * kfield[0]
    other_g = gfield[1] - ratio * gfield[0]
    other_a = second_a - ratio * cross_k
    other_q = second_g - 2.0 * ratio * cross_g + ratio * ratio * first_g
    first_mu = first_g / first_a
    other_mu = other_q / other_a
    new_first = (field[0] + step_size * precond * (gfield[0] - first_mu * kfield[0])) * jnp.sqrt(norm_scale * cells / first_a)
    new_other = (other + step_size * precond * (other_g - other_mu * other_k)) * jnp.sqrt(norm_scale * cells / other_a)
    return jnp.stack([new_first, new_other])

def reference(vectors, prestress, thickness, foundation, patch_rows, matched, elem_row):
    placed = jnp.zeros((ROWS, 3, C), jnp.bfloat16).at[elem_row].set(prestress)
    stress = placed.astype(jnp.float32).reshape(PATCHES, PROWS, 3, C)
    rows = jnp.arange(PROWS, dtype=jnp.int32)[None, :]
    live = (rows < patch_rows[:, None]).astype(jnp.float32)[:, :, None]
    thick = thickness.reshape(PATCHES, PROWS, C)
    support = foundation.reshape(PATCHES, PROWS, C)
    precond = live / (support + 12.0 * thick)
    inverse = jnp.zeros((PATCHES,), jnp.int32).at[matched].set(jnp.arange(PATCHES, dtype=jnp.int32))
    field = vectors.reshape(2, PATCHES, PROWS, C) * live
    cells = jnp.float32(ROWS * C)
    for step in range(ITERS):
        top, bottom = edges(field, patch_rows)
        partner_bottom = bottom[:, matched]
        partner_top = top[:, inverse]
        kfield = stiffness(field, live, thick, support) + interface(field, patch_rows, top, bottom, partner_top, partner_bottom)
        gfield = geometric(field, live, stress)
        totals = products(field, kfield, gfield)
        field = advance(field, kfield, gfield, totals, precond, cells)
    return field.reshape(2, ROWS, C)
```

```python
import jax
import jax.numpy as jnp
from jax import lax
from jax.experimental import pallas as pl
from jax.experimental.pallas import tpu as pltpu
from jax.sharding import PartitionSpec as P

step_size = 1.0
norm_scale = 16.0
penalty_value = 8.0
penalty_slope = 4.0

MESH = pl.DeviceIdType.MESH
PAD = 8
LANES = 128
CHUNK = 32


def body(
    vec, pre, thick_in, found_in, lengths, matched, elem, out,
    x, thick, found, prec, stress, mrow, frow, kpart, gpart, kf, gf,
    arrived, ids, strips, got, edge, sums, coef,
    load_sem, own_sem, data_send, data_recv, ids_send, ids_recv,
    strip_send, strip_recv, sum_send, sum_recv,
):
    owners, subs, halves = (lax.axis_size(a) for a in ("patch", "sub", "half"))
    n = owners * subs * halves
    pi, si, hi = (lax.axis_index(a) for a in ("patch", "sub", "half"))
    me = (pi * subs + si) * halves + hi
    slots = x.shape[1]
    prows = x.shape[2] - 2 * PAD
    ncol = x.shape[3]
    rows_dev = slots * prows
    per_peer = rows_dev // n
    chunk = CHUNK
    per_slot = prows // chunk
    steps = slots * per_slot

    def peer(d):
        k = lax.rem(me + d, n)
        where = {
            "patch": lax.div(k, subs * halves),
            "sub": lax.rem(lax.div(k, halves), subs),
            "half": lax.rem(k, halves),
        }
        return k, where

    barrier = pltpu.get_barrier_semaphore()

    @pl.loop(1, n)
    def _(d):
        _, where = peer(d)
        pl.semaphore_signal(barrier, inc=1, device_id=where, device_id_type=MESH)

    loads = []
    for v in range(2):
        for s in range(slots):
            loads.append(
                pltpu.make_async_copy(
                    vec.at[v, pl.ds(s * prows, prows)],
                    x.at[v, s, pl.ds(PAD, prows)],
                    load_sem.at[v * slots + s],
                )
            )
    load_thick = pltpu.make_async_copy(thick_in, thick, load_sem.at[2 * slots])
    load_found = pltpu.make_async_copy(found_in, found, load_sem.at[2 * slots + 1])
    own_data = pltpu.make_async_copy(pre.at[:, me], arrived.at[:, me], own_sem.at[0])
    own_ids = pltpu.make_async_copy(elem, ids.at[me], own_sem.at[1])
    for copy in loads + [load_thick, load_found, own_data, own_ids]:
        copy.start()

    zero_pad = jnp.zeros((PAD, ncol), jnp.float32)
    for v in range(2):
        for s in range(slots):
            for ref in (x, mrow, frow):
                ref[v, s, 0:PAD, :] = zero_pad
                ref[v, s, PAD + prows : 2 * PAD + prows, :] = zero_pad
    for copy in loads:
        copy.wait()

    def fill_strip(which, row_of):
        for s in range(slots):
            length = jnp.maximum(lengths[s], 2)
            for v in range(2):
                base = (s * 2 + v) * 4
                for r, at in enumerate((length - 2, length - 1, 0, 1)):
                    strips[which, base + r : base + r + 1, :] = row_of(s, v, at)

    rows_strip = slots * 2 * 4
    fill_strip(0, lambda s, v, at: x[v, s, pl.ds(PAD + at, 1), :])
    for s in range(slots):
        strips[0, rows_strip + s : rows_strip + s + 1, :] = jnp.full(
            (1, ncol), matched[s], jnp.int32
        ).astype(jnp.float32)

    pl.semaphore_wait(barrier, n - 1)

    def strip_copies(which, rows):
        copies = []
        for side, by in ((0, 1), (1, owners - 1)):
            copies.append(
                pltpu.make_async_remote_copy(
                    src_ref=strips.at[which, pl.ds(0, rows)],
                    dst_ref=got.at[which, side, pl.ds(0, rows)],
                    send_sem=strip_send.at[which * 2 + side],
                    recv_sem=strip_recv.at[which * 2 + side],
                    device_id={"patch": lax.rem(pi + by, owners)},
                    device_id_type=MESH,
                )
            )
        return copies

    first_strips = strip_copies(0, strips.shape[1])
    for copy in first_strips:
        copy.start()

    @pl.loop(1, n)
    def _(d):
        k, where = peer(d)
        pltpu.make_async_remote_copy(
            src_ref=elem, dst_ref=ids.at[me], send_sem=ids_send.at[0],
            recv_sem=ids_recv.at[0], device_id=where, device_id_type=MESH,
        ).start()
        pltpu.make_async_remote_copy(
            src_ref=pre.at[:, k], dst_ref=arrived.at[:, me], send_sem=data_send.at[0],
            recv_sem=data_recv.at[0], device_id=where, device_id_type=MESH,
        ).start()

    def all_ids():
        part = ids.at[pl.ds(0, n - 1)]
        return pltpu.make_async_remote_copy(
            src_ref=part, dst_ref=part, send_sem=ids_send.at[0], recv_sem=ids_recv.at[0],
            device_id={"patch": pi}, device_id_type=MESH,
        )

    def all_data():
        part = arrived.at[:, pl.ds(0, n - 1)]
        return pltpu.make_async_remote_copy(
            src_ref=part, dst_ref=part, send_sem=data_send.at[0], recv_sem=data_recv.at[0],
            device_id={"patch": pi}, device_id_type=MESH,
        )

    lane = lax.broadcasted_iota(jnp.int32, (chunk, ncol), 1)
    first_lane = lane == 0
    last_lane = lane == ncol - 1
    sub_row = lax.broadcasted_iota(jnp.int32, (chunk, ncol), 0)

    def before(w):
        return jnp.where(first_lane, 0.0, pltpu.roll(w, 1, 1))

    def after(w):
        return jnp.where(last_lane, 0.0, pltpu.roll(w, ncol - 1, 1))

    def place(i):
        s = lax.div(i, per_slot)
        r0 = pl.multiple_of(lax.rem(i, per_slot) * chunk, chunk)
        full = pl.multiple_of(i * chunk, chunk)
        return s, r0, pl.ds(full, chunk), r0 + sub_row, lengths[s]

    def shifted(ref, v, s, r0, by):
        window = ref.at[v, s, pl.ds(r0, chunk + 2 * PAD)]
        return window[PAD + by : PAD + by + chunk, :]

    load_thick.wait()
    load_found.wait()

    @pl.loop(0, steps)
    def _(i):
        s, r0, full, row, length = place(i)
        live = row < length
        for v in range(2):
            at = pl.ds(r0 + PAD, chunk)
            x[v, s, at, :] = jnp.where(live, x[v, s, at, :], 0.0)
        prec[full, :] = jnp.where(live, 1.0, 0.0) / (found[full, :] + 12.0 * thick[full, :])

    def stiff_first(i):
        s, r0, full, row, length = place(i)
        th = thick[full, :]
        fo = found[full, :]
        live_th = jnp.where(row < length, th, 0.0)
        for v in range(2):
            w = shifted(x, v, s, r0, 0)
            mrow[v, s, pl.ds(r0 + PAD, chunk), :] = live_th * (
                shifted(x, v, s, r0, -1) - 2.0 * w + shifted(x, v, s, r0, 1)
            )
            bend = th * (before(w) - 2.0 * w + after(w))
            kpart[v, full, :] = fo * w + (before(bend) - 2.0 * bend + after(bend))

    def geo_first(i):
        s, r0, full, row, length = place(i)
        nuu = stress[0, full, :]
        nvv = stress[1, full, :]
        nuv = stress[2, full, :]
        for v in range(2):
            w = shifted(x, v, s, r0, 0)
            along_rows = shifted(x, v, s, r0, 1) - w
            along_cols = after(w) - w
            frow[v, s, pl.ds(r0 + PAD, chunk), :] = nuu * along_rows + nuv * along_cols
            cols = nvv * along_cols + nuv * along_rows
            gpart[v, full, :] = before(cols) - cols

    def fold(value):
        total = value[0:8]
        for j in range(8, chunk, 8):
            total = total + value[j : j + 8]
        return total

    def stiff_second(i, acc):
        s, r0, full, row, length = place(i)
        ks = []
        for v in range(2):
            m = shifted(mrow, v, s, r0, 0)
            bent = shifted(mrow, v, s, r0, -1) - 2.0 * m + shifted(mrow, v, s, r0, 1)
            k = jnp.where(row < length, kpart[v, full, :] + bent, 0.0)

            def line(r):
                return edge[s, v, r : r + 1, :]

            joint = jnp.where(row == length - 1, line(0), 0.0)
            joint = jnp.where(row == length - 2, line(1), joint)
            joint = jnp.where(row == 0, line(2), joint)
            joint = jnp.where(row == 1, line(3), joint)
            k = k + joint
            kf[v, full, :] = k
            ks.append(k)
        x0 = shifted(x, 0, s, r0, 0)
        x1 = shifted(x, 1, s, r0, 0)
        return (
            acc[0] + fold(x0 * ks[0]),
            acc[1] + fold(x0 * ks[1]),
            acc[2] + fold(x1 * ks[1]),
        )

    def geo_second(i, acc):
        s, r0, full, row, length = place(i)
        gs = []
        for v in range(2):
            g = shifted(frow, v, s, r0, -1) - shifted(frow, v, s, r0, 0) + gpart[v, full, :]
            g = jnp.where(row < length, g, 0.0)
            gf[v, full, :] = g
            gs.append(g)
        x0 = shifted(x, 0, s, r0, 0)
        x1 = shifted(x, 1, s, r0, 0)
        return (
            acc[0] + fold(x0 * gs[0]),
            acc[1] + fold(x0 * gs[1]),
            acc[2] + fold(x1 * gs[1]),
        )

    def chosen(which, v, s):
        wanted = jnp.full((2, ncol), matched[s], jnp.int32)
        mine = (me * slots + s).astype(jnp.float32)
        bottom = jnp.zeros((2, ncol), jnp.float32)
        top = jnp.zeros((2, ncol), jnp.float32)
        for side, by in ((0, owners - 1), (1, 1)):
            other = (lax.rem(pi + by, owners) * subs + si) * halves + hi
            for t in range(slots):
                base = (t * 2 + v) * 4
                bottom = bottom + jnp.where(
                    wanted == other * slots + t, got[which, side, base + 2 : base + 4, :], 0.0
                )
                label = got[0, side, rows_strip + t : rows_strip + t + 1, :]
                top = top + jnp.where(label == mine, got[which, side, base : base + 2, :], 0.0)
        return top, bottom

    def set_edge(s, v, partner_top, partner_bottom):
        length = jnp.maximum(lengths[s], 2)
        top0 = x[v, s, pl.ds(PAD + length - 2, 1), :]
        top1 = x[v, s, pl.ds(PAD + length - 1, 1), :]
        bot0 = x[v, s, PAD : PAD + 1, :]
        bot1 = x[v, s, PAD + 1 : PAD + 2, :]
        ptop0, ptop1 = partner_top[0:1], partner_top[1:2]
        pbot0, pbot1 = partner_bottom[0:1], partner_bottom[1:2]
        jump_top = top1 - pbot0
        slope_top = top1 - top0 - (pbot1 - pbot0)
        jump_bottom = ptop1 - bot0
        slope_bottom = ptop1 - ptop0 - (bot1 - bot0)
        edge[s, v, 0:1, :] = penalty_value * jump_top + penalty_slope * slope_top
        edge[s, v, 1:2, :] = -penalty_slope * slope_top
        edge[s, v, 2:3, :] = -penalty_value * jump_bottom + penalty_slope * slope_bottom
        edge[s, v, 3:4, :] = -penalty_slope * slope_bottom

    def sum_copy(it, where):
        return pltpu.make_async_remote_copy(
            src_ref=sums.at[it, me], dst_ref=sums.at[it, me], send_sem=sum_send.at[it],
            recv_sem=sum_recv.at[it], device_id=where, device_id_type=MESH,
        )

    def all_sums(it):
        part = sums.at[it, pl.ds(0, n - 1)]
        return pltpu.make_async_remote_copy(
            src_ref=part, dst_ref=part, send_sem=sum_send.at[it], recv_sem=sum_recv.at[it],
            device_id={"patch": pi}, device_id_type=MESH,
        )

    def send_sums(it, totals):
        spot = lax.broadcasted_iota(jnp.int32, (1, LANES), 1)
        line = jnp.zeros((1, LANES), jnp.float32)
        for t, total in enumerate(totals):
            one = jnp.sum(jnp.sum(total, axis=0, keepdims=True), axis=1, keepdims=True)
            line = jnp.where(spot == t, one, line)
        sums[it, me] = line

        @pl.loop(1, n)
        def _(d):
            _, where = peer(d)
            sum_copy(it, where).start()

    def read_sums(it):
        all_sums(it).wait_recv()
        line = jnp.sum(sums[it], axis=0)
        first_a, cross_k, second_a, first_g, cross_g, second_g = (
            line[:, t : t + 1] for t in range(6)
        )
        cells = float(n * rows_dev * ncol)
        ratio = cross_k / first_a
        other_a = second_a - ratio * cross_k
        other_q = second_g - 2.0 * ratio * cross_g + ratio * ratio * first_g
        values = (
            ratio,
            first_g / first_a,
            other_q / other_a,
            jnp.sqrt(norm_scale * cells / first_a),
            jnp.sqrt(norm_scale * cells / other_a),
        )
        for t, value in enumerate(values):
            coef[t : t + 1, :] = jnp.broadcast_to(value, (1, ncol))

    def stepped(x0, x1, pk0, pk1, pg0, pg1):
        ratio, mu1, mu2, scale0, scale1 = (coef[t : t + 1, :] for t in range(5))
        new0 = (x0 + step_size * (pg0 - mu1 * pk0)) * scale0
        new1 = (
            (x1 - ratio * x0) + step_size * ((pg1 - ratio * pg0) - mu2 * (pk1 - ratio * pk0))
        ) * scale1
        return new0, new1

    def advanced(i):
        s, r0, full, row, length = place(i)
        ratio, mu1, mu2, scale0, scale1 = (coef[t : t + 1, :] for t in range(5))
        p = step_size * prec[full, :]
        x0 = shifted(x, 0, s, r0, 0)
        k0 = kf[0, full, :]
        g0 = gf[0, full, :]
        new0 = (x0 + p * (g0 - mu1 * k0)) * scale0
        y = shifted(x, 1, s, r0, 0) - ratio * x0
        ky = kf[1, full, :] - ratio * k0
        gy = gf[1, full, :] - ratio * g0
        new1 = (y + p * (gy - mu2 * ky)) * scale1
        return s, r0, full, new0, new1

    nothing = tuple(jnp.zeros((8, ncol), jnp.float32) for _ in range(3))

    pl.loop(0, steps)(stiff_first)
    for copy in first_strips:
        copy.wait_recv()
    for s in range(slots):
        for v in range(2):
            set_edge(s, v, *chosen(0, v, s))
    k_sums = lax.fori_loop(0, steps, stiff_second, nothing)

    def scaled_row(ref):
        def pick(s, v, at):
            spot = pl.ds(s * prows + at, 1)
            return prec[spot, :] * ref[v, spot, :]

        return pick

    fill_strip(1, scaled_row(kf))
    second_strips = strip_copies(1, rows_strip)
    for copy in second_strips:
        copy.start()

    own_ids.wait()
    all_ids().wait_recv()
    who = jnp.broadcast_to(ids[...], (n, per_peer, ncol)).reshape(rows_dev, ncol)
    wide_lane = lax.broadcasted_iota(jnp.int32, (rows_dev, ncol), 1)
    wide_row = lax.broadcasted_iota(jnp.int32, (rows_dev, ncol), 0)
    pick = wide_lane == me * per_peer + lax.rem(wide_row, per_peer)
    target = lax.rem(
        jnp.sum(jnp.where(pick, who, 0).astype(jnp.float32), axis=1, keepdims=True).astype(jnp.int32),
        rows_dev,
    )
    to = lax.broadcasted_iota(jnp.int32, (rows_dev, rows_dev), 1)
    onehot = (to == target).astype(jnp.float32).astype(jnp.bfloat16)

    own_data.wait()
    all_data().wait_recv()
    for c in range(3):
        block = arrived[c]
        if per_peer % 8:
            block = block.astype(jnp.float32).reshape(rows_dev, ncol).astype(jnp.bfloat16)
        else:
            block = block.reshape(rows_dev, ncol)
        stress[c] = lax.dot_general(
            onehot, block, (((0,), (0,)), ((), ())), preferred_element_type=jnp.float32
        )

    pl.loop(0, steps)(geo_first)
    g_sums = lax.fori_loop(0, steps, geo_second, nothing)
    send_sums(0, k_sums + g_sums)
    fill_strip(2, scaled_row(gf))
    third_strips = strip_copies(2, rows_strip)
    for copy in third_strips:
        copy.start()

    read_sums(0)

    @pl.loop(0, steps)
    def _(i):
        s, r0, full, new0, new1 = advanced(i)
        x[0, s, pl.ds(r0 + PAD, chunk), :] = new0
        x[1, s, pl.ds(r0 + PAD, chunk), :] = new1

    @pl.loop(0, steps)
    def _(i):
        stiff_first(i)
        geo_first(i)

    for copy in second_strips + third_strips:
        copy.wait_recv()
    for s in range(slots):
        parts = [[chosen(which, v, s) for v in range(2)] for which in range(3)]
        ends = []
        for end in range(2):
            ends.append(stepped(*(parts[which][v][end] for which in range(3) for v in range(2))))
        for v in range(2):
            set_edge(s, v, ends[0][v], ends[1][v])

    def second(i, acc):
        return stiff_second(i, acc[:3]) + geo_second(i, acc[3:])

    totals = lax.fori_loop(0, steps, second, nothing + nothing)
    send_sums(1, totals)
    read_sums(1)

    @pl.loop(0, steps)
    def _(i):
        s, r0, full, new0, new1 = advanced(i)
        out[0, full, :] = new0
        out[1, full, :] = new1

    for copy in first_strips + second_strips + third_strips:
        copy.wait_send()
    all_ids().wait_send()
    all_data().wait_send()
    all_sums(0).wait_send()
    all_sums(1).wait_send()


def per_device(vectors, prestress, thickness, foundation, patch_rows, matched, elem_row):
    n = lax.axis_size(("patch", "sub", "half"))
    slots = patch_rows.shape[0]
    rows_dev, ncol = thickness.shape
    prows = rows_dev // slots
    per_peer = rows_dev // n
    pre = jnp.transpose(prestress, (1, 0, 2)).reshape(3, n, per_peer, ncol)
    elem = elem_row.reshape(1, rows_dev)
    f32 = jnp.float32
    padded = pltpu.VMEM((2, slots, prows + 2 * PAD, ncol), f32)
    flat = pltpu.VMEM((rows_dev, ncol), f32)
    pair = pltpu.VMEM((2, rows_dev, ncol), f32)
    strip_rows = slots * 8 + -(-slots // 8) * 8
    anywhere = pl.BlockSpec(memory_space=pl.ANY)
    scalars = pl.BlockSpec(memory_space=pltpu.SMEM)
    dma = pltpu.SemaphoreType.DMA
    return pl.pallas_call(
        body,
        out_shape=jax.ShapeDtypeStruct((2, rows_dev, ncol), f32),
        in_specs=[anywhere] * 4 + [scalars] * 2 + [anywhere],
        out_specs=pl.BlockSpec(memory_space=pltpu.VMEM),
        scratch_shapes=[
            padded, flat, flat, flat,
            pltpu.VMEM((3, rows_dev, ncol), f32),
            padded, padded, pair, pair, pair, pair,
            pltpu.VMEM((3, n, per_peer, ncol), jnp.bfloat16),
            pltpu.VMEM((n, 1, rows_dev), jnp.int32),
            pltpu.VMEM((3, strip_rows, ncol), f32),
            pltpu.VMEM((3, 2, strip_rows, ncol), f32),
            pltpu.VMEM((slots, 2, 8, ncol), f32),
            pltpu.VMEM((2, n, 1, LANES), f32),
            pltpu.VMEM((8, ncol), f32),
            dma((2 * slots + 2,)), dma((2,)),
            dma((1,)), dma((1,)), dma((1,)), dma((1,)),
            dma((6,)), dma((6,)), dma((2,)), dma((2,)),
        ],
        compiler_params=pltpu.CompilerParams(
            collective_id=0, has_side_effects=True, vmem_limit_bytes=24 << 20
        ),
    )(vectors, pre, thickness, foundation, patch_rows, matched, elem)


def solution(mesh):
    split = ("groups", "patch", "sub", "half")
    in_specs = (
        P(None, split, None),
        P(split, None, None),
        P(split, None),
        P(split, None),
        P(split),
        P(split),
        P(split),
    )
    return jax.shard_map(
        per_device, mesh=mesh, in_specs=in_specs, out_specs=P(None, split, None), check_vma=False
    )
```

```python
import jax
import jax.numpy as jnp
from jax import lax
from jax.experimental import pallas as pl
from jax.experimental.pallas import tpu as pltpu
from jax.sharding import PartitionSpec as P

step_size = 1.0
norm_scale = 16.0
penalty_value = 8.0
penalty_slope = 4.0

MESH = pl.DeviceIdType.MESH
PAD = 8
LANES = 128
CHUNK = 128


def body(
    vec, pre, thick_in, found_in, lengths_in, matched_in, elem, out,
    lengths, matched,
    x, thick, found, prec, stress, mrow, frow, kpart, gpart, kf, gf,
    arrived, ids, strips, got, edge, sums, coef,
    load_sem, own_sem, data_send, data_recv, ids_send, ids_recv,
    strip_send, strip_recv, sum_send, sum_recv,
):
    owners, subs, halves = (lax.axis_size(a) for a in ("patch", "sub", "half"))
    n = owners * subs * halves
    pi, si, hi = (lax.axis_index(a) for a in ("patch", "sub", "half"))
    me = (pi * subs + si) * halves + hi
    slots = x.shape[1]
    prows = x.shape[2] - 2 * PAD
    ncol = x.shape[3]
    rows_dev = slots * prows
    per_peer = rows_dev // n
    chunk = CHUNK
    per_slot = prows // chunk
    steps = slots * per_slot

    ends_of = 2 if owners % 2 == 0 else 1
    near = owners // ends_of

    def peer(d):
        step = lax.rem(d + (n // 2 if ends_of == 2 else 0), n)
        side = lax.rem(lax.div(pi, near) + lax.div(step, near * subs * halves), ends_of)
        along = lax.rem(lax.rem(pi, near) + lax.rem(lax.div(step, subs * halves), near), near)
        to_patch = side * near + along
        to_sub = lax.rem(si + lax.rem(lax.div(step, halves), subs), subs)
        to_half = lax.rem(hi + lax.rem(step, halves), halves)
        k = (to_patch * subs + to_sub) * halves + to_half
        return k, {"patch": to_patch, "sub": to_sub, "half": to_half}

    def for_peers(action):
        start = n // 2 if ends_of == 2 else 0

        def one(e):
            d = lax.select(e < start, e, e + 1) if start else e + 1
            action(*peer(d))

        if n <= 16:
            for e in range(n - 1):
                one(jnp.int32(e))
        else:
            pl.loop(0, n - 1)(one)

    barrier = pltpu.get_barrier_semaphore()

    def greet(k, where):
        pl.semaphore_signal(barrier, inc=1, device_id=where, device_id_type=MESH)

    for_peers(greet)

    loads = []
    for v in range(2):
        for s in range(slots):
            loads.append(
                pltpu.make_async_copy(
                    vec.at[v, pl.ds(s * prows, prows)],
                    x.at[v, s, pl.ds(PAD, prows)],
                    load_sem.at[v * slots + s],
                )
            )
    load_thick = pltpu.make_async_copy(thick_in, thick, load_sem.at[2 * slots])
    load_found = pltpu.make_async_copy(found_in, found, load_sem.at[2 * slots + 1])
    own_data = pltpu.make_async_copy(pre.at[:, me], arrived.at[:, me], own_sem.at[0])
    own_ids = pltpu.make_async_copy(elem, ids.at[me], own_sem.at[1])
    load_ints = [
        pltpu.make_async_copy(lengths_in, lengths, own_sem.at[2]),
        pltpu.make_async_copy(matched_in, matched, own_sem.at[3]),
    ]
    for copy in load_ints + loads + [load_thick, load_found, own_data, own_ids]:
        copy.start()

    zero_pad = jnp.zeros((PAD, ncol), jnp.float32)
    for v in range(2):
        for s in range(slots):
            for ref in (x, mrow, frow):
                ref[v, s, 0:PAD, :] = zero_pad
                ref[v, s, PAD + prows : 2 * PAD + prows, :] = zero_pad
    for copy in load_ints + loads:
        copy.wait()

    def fill_strip(which, row_of):
        for s in range(slots):
            length = jnp.maximum(lengths[s], 2)
            for v in range(2):
                base = (s * 2 + v) * 4
                for r, at in enumerate((length - 2, length - 1, 0, 1)):
                    strips[which, base + r : base + r + 1, :] = row_of(s, v, at)

    rows_strip = slots * 2 * 4
    fill_strip(0, lambda s, v, at: x[v, s, pl.ds(PAD + at, 1), :])
    for s in range(slots):
        strips[0, rows_strip + s : rows_strip + s + 1, :] = jnp.full(
            (1, ncol), matched[s], jnp.int32
        ).astype(jnp.float32)

    pl.semaphore_wait(barrier, n - 1)

    def strip_copies(which, rows):
        copies = []
        for side, by in ((0, 1), (1, owners - 1)):
            copies.append(
                pltpu.make_async_remote_copy(
                    src_ref=strips.at[which, pl.ds(0, rows)],
                    dst_ref=got.at[which, side, pl.ds(0, rows)],
                    send_sem=strip_send.at[which * 2 + side],
                    recv_sem=strip_recv.at[which * 2 + side],
                    device_id={"patch": lax.rem(pi + by, owners)},
                    device_id_type=MESH,
                )
            )
        return copies

    first_strips = strip_copies(0, strips.shape[1])
    for copy in first_strips:
        copy.start()

    def send_block(k, where):
        pltpu.make_async_remote_copy(
            src_ref=elem, dst_ref=ids.at[me], send_sem=ids_send.at[0],
            recv_sem=ids_recv.at[0], device_id=where, device_id_type=MESH,
        ).start()
        pltpu.make_async_remote_copy(
            src_ref=pre.at[:, k], dst_ref=arrived.at[:, me], send_sem=data_send.at[0],
            recv_sem=data_recv.at[0], device_id=where, device_id_type=MESH,
        ).start()

    for_peers(send_block)

    def all_ids():
        part = ids.at[pl.ds(0, n - 1)]
        return pltpu.make_async_remote_copy(
            src_ref=part, dst_ref=part, send_sem=ids_send.at[0], recv_sem=ids_recv.at[0],
            device_id={"patch": pi}, device_id_type=MESH,
        )

    def all_data():
        part = arrived.at[:, pl.ds(0, n - 1)]
        return pltpu.make_async_remote_copy(
            src_ref=part, dst_ref=part, send_sem=data_send.at[0], recv_sem=data_recv.at[0],
            device_id={"patch": pi}, device_id_type=MESH,
        )

    lane = lax.broadcasted_iota(jnp.int32, (chunk, ncol), 1)
    first_lane = lane == 0
    last_lane = lane == ncol - 1
    sub_row = lax.broadcasted_iota(jnp.int32, (chunk, ncol), 0)

    def before(w):
        return jnp.where(first_lane, 0.0, pltpu.roll(w, 1, 1))

    def after(w):
        return jnp.where(last_lane, 0.0, pltpu.roll(w, ncol - 1, 1))

    def place(i):
        s = lax.div(i, per_slot)
        r0 = pl.multiple_of(lax.rem(i, per_slot) * chunk, chunk)
        full = pl.multiple_of(i * chunk, chunk)
        return s, r0, pl.ds(full, chunk), r0 + sub_row, lengths[s]

    def shifted(ref, v, s, r0, by):
        window = ref.at[v, s, pl.ds(r0, chunk + 2 * PAD)]
        return window[PAD + by : PAD + by + chunk, :]

    load_thick.wait()
    load_found.wait()

    @pl.loop(0, steps)
    def _(i):
        s, r0, full, row, length = place(i)
        live = row < length
        for v in range(2):
            at = pl.ds(r0 + PAD, chunk)
            x[v, s, at, :] = jnp.where(live, x[v, s, at, :], 0.0)
        prec[full, :] = jnp.where(live, 1.0, 0.0) / (found[full, :] + 12.0 * thick[full, :])

    def stiff_first(i):
        s, r0, full, row, length = place(i)
        th = thick[full, :]
        fo = found[full, :]
        live_th = jnp.where(row < length, th, 0.0)
        for v in range(2):
            w = shifted(x, v, s, r0, 0)
            mrow[v, s, pl.ds(r0 + PAD, chunk), :] = live_th * (
                shifted(x, v, s, r0, -1) - 2.0 * w + shifted(x, v, s, r0, 1)
            )
            bend = th * (before(w) - 2.0 * w + after(w))
            kpart[v, full, :] = fo * w + (before(bend) - 2.0 * bend + after(bend))

    def geo_first(i):
        s, r0, full, row, length = place(i)
        nuu = stress[0, full, :]
        nvv = stress[1, full, :]
        nuv = stress[2, full, :]
        for v in range(2):
            w = shifted(x, v, s, r0, 0)
            along_rows = shifted(x, v, s, r0, 1) - w
            along_cols = after(w) - w
            frow[v, s, pl.ds(r0 + PAD, chunk), :] = nuu * along_rows + nuv * along_cols
            cols = nvv * along_cols + nuv * along_rows
            gpart[v, full, :] = before(cols) - cols

    def fold(value):
        total = value[0:8]
        for j in range(8, chunk, 8):
            total = total + value[j : j + 8]
        return total

    def stiff_second(i, acc):
        s, r0, full, row, length = place(i)
        ks = []
        for v in range(2):
            m = shifted(mrow, v, s, r0, 0)
            bent = shifted(mrow, v, s, r0, -1) - 2.0 * m + shifted(mrow, v, s, r0, 1)
            k = jnp.where(row < length, kpart[v, full, :] + bent, 0.0)

            def line(r):
                return edge[s, v, r : r + 1, :]

            joint = jnp.where(row == length - 1, line(0), 0.0)
            joint = jnp.where(row == length - 2, line(1), joint)
            joint = jnp.where(row == 0, line(2), joint)
            joint = jnp.where(row == 1, line(3), joint)
            k = k + joint
            kf[v, full, :] = k
            ks.append(k)
        x0 = shifted(x, 0, s, r0, 0)
        x1 = shifted(x, 1, s, r0, 0)
        return (
            acc[0] + fold(x0 * ks[0]),
            acc[1] + fold(x0 * ks[1]),
            acc[2] + fold(x1 * ks[1]),
        )

    def geo_second(i, acc):
        s, r0, full, row, length = place(i)
        gs = []
        for v in range(2):
            g = shifted(frow, v, s, r0, -1) - shifted(frow, v, s, r0, 0) + gpart[v, full, :]
            g = jnp.where(row < length, g, 0.0)
            gf[v, full, :] = g
            gs.append(g)
        x0 = shifted(x, 0, s, r0, 0)
        x1 = shifted(x, 1, s, r0, 0)
        return (
            acc[0] + fold(x0 * gs[0]),
            acc[1] + fold(x0 * gs[1]),
            acc[2] + fold(x1 * gs[1]),
        )

    def chosen(which, v, s):
        wanted = jnp.full((2, ncol), matched[s], jnp.int32)
        mine = (me * slots + s).astype(jnp.float32)
        bottom = jnp.zeros((2, ncol), jnp.float32)
        top = jnp.zeros((2, ncol), jnp.float32)
        for side, by in ((0, owners - 1), (1, 1)):
            other = (lax.rem(pi + by, owners) * subs + si) * halves + hi
            for t in range(slots):
                base = (t * 2 + v) * 4
                bottom = bottom + jnp.where(
                    wanted == other * slots + t, got[which, side, base + 2 : base + 4, :], 0.0
                )
                label = got[0, side, rows_strip + t : rows_strip + t + 1, :]
                top = top + jnp.where(label == mine, got[which, side, base : base + 2, :], 0.0)
        return top, bottom

    def set_edge(s, v, partner_top, partner_bottom):
        length = jnp.maximum(lengths[s], 2)
        top0 = x[v, s, pl.ds(PAD + length - 2, 1), :]
        top1 = x[v, s, pl.ds(PAD + length - 1, 1), :]
        bot0 = x[v, s, PAD : PAD + 1, :]
        bot1 = x[v, s, PAD + 1 : PAD + 2, :]
        ptop0, ptop1 = partner_top[0:1], partner_top[1:2]
        pbot0, pbot1 = partner_bottom[0:1], partner_bottom[1:2]
        jump_top = top1 - pbot0
        slope_top = top1 - top0 - (pbot1 - pbot0)
        jump_bottom = ptop1 - bot0
        slope_bottom = ptop1 - ptop0 - (bot1 - bot0)
        edge[s, v, 0:1, :] = penalty_value * jump_top + penalty_slope * slope_top
        edge[s, v, 1:2, :] = -penalty_slope * slope_top
        edge[s, v, 2:3, :] = -penalty_value * jump_bottom + penalty_slope * slope_bottom
        edge[s, v, 3:4, :] = -penalty_slope * slope_bottom

    def sum_copy(it, where):
        return pltpu.make_async_remote_copy(
            src_ref=sums.at[it, me], dst_ref=sums.at[it, me], send_sem=sum_send.at[it],
            recv_sem=sum_recv.at[it], device_id=where, device_id_type=MESH,
        )

    def all_sums(it):
        part = sums.at[it, pl.ds(0, n - 1)]
        return pltpu.make_async_remote_copy(
            src_ref=part, dst_ref=part, send_sem=sum_send.at[it], recv_sem=sum_recv.at[it],
            device_id={"patch": pi}, device_id_type=MESH,
        )

    def send_sums(it, totals):
        spot = lax.broadcasted_iota(jnp.int32, (1, LANES), 1)
        line = jnp.zeros((1, LANES), jnp.float32)
        for t, total in enumerate(totals):
            one = jnp.sum(jnp.sum(total, axis=0, keepdims=True), axis=1, keepdims=True)
            line = jnp.where(spot == t, one, line)
        sums[it, me] = line

        def send_line(k, where):
            sum_copy(it, where).start()

        for_peers(send_line)

    def read_sums(it):
        all_sums(it).wait_recv()
        line = jnp.sum(sums[it], axis=0)
        first_a, cross_k, second_a, first_g, cross_g, second_g = (
            line[:, t : t + 1] for t in range(6)
        )
        cells = float(n * rows_dev * ncol)
        ratio = cross_k / first_a
        other_a = second_a - ratio * cross_k
        other_q = second_g - 2.0 * ratio * cross_g + ratio * ratio * first_g
        values = (
            ratio,
            first_g / first_a,
            other_q / other_a,
            jnp.sqrt(norm_scale * cells / first_a),
            jnp.sqrt(norm_scale * cells / other_a),
        )
        for t, value in enumerate(values):
            coef[t : t + 1, :] = jnp.broadcast_to(value, (1, ncol))

    def stepped(x0, x1, pk0, pk1, pg0, pg1):
        ratio, mu1, mu2, scale0, scale1 = (coef[t : t + 1, :] for t in range(5))
        new0 = (x0 + step_size * (pg0 - mu1 * pk0)) * scale0
        new1 = (
            (x1 - ratio * x0) + step_size * ((pg1 - ratio * pg0) - mu2 * (pk1 - ratio * pk0))
        ) * scale1
        return new0, new1

    def advanced(i):
        s, r0, full, row, length = place(i)
        ratio, mu1, mu2, scale0, scale1 = (coef[t : t + 1, :] for t in range(5))
        p = step_size * prec[full, :]
        x0 = shifted(x, 0, s, r0, 0)
        k0 = kf[0, full, :]
        g0 = gf[0, full, :]
        new0 = (x0 + p * (g0 - mu1 * k0)) * scale0
        y = shifted(x, 1, s, r0, 0) - ratio * x0
        ky = kf[1, full, :] - ratio * k0
        gy = gf[1, full, :] - ratio * g0
        new1 = (y + p * (gy - mu2 * ky)) * scale1
        return s, r0, full, new0, new1

    nothing = tuple(jnp.zeros((8, ncol), jnp.float32) for _ in range(3))

    pl.loop(0, steps)(stiff_first)
    for copy in first_strips:
        copy.wait_recv()
    for s in range(slots):
        for v in range(2):
            set_edge(s, v, *chosen(0, v, s))
    k_sums = lax.fori_loop(0, steps, stiff_second, nothing)

    def scaled_row(ref):
        def pick(s, v, at):
            spot = pl.ds(s * prows + at, 1)
            return prec[spot, :] * ref[v, spot, :]

        return pick

    fill_strip(1, scaled_row(kf))
    second_strips = strip_copies(1, rows_strip)
    for copy in second_strips:
        copy.start()

    own_ids.wait()
    all_ids().wait_recv()
    who = jnp.broadcast_to(ids[...], (n, per_peer, ncol)).reshape(rows_dev, ncol)
    wide_lane = lax.broadcasted_iota(jnp.int32, (rows_dev, ncol), 1)
    wide_row = lax.broadcasted_iota(jnp.int32, (rows_dev, ncol), 0)
    pick = wide_lane == me * per_peer + lax.rem(wide_row, per_peer)
    target = lax.rem(
        jnp.sum(jnp.where(pick, who, 0).astype(jnp.float32), axis=1, keepdims=True).astype(jnp.int32),
        rows_dev,
    )
    to = lax.broadcasted_iota(jnp.int32, (rows_dev, rows_dev), 1)
    onehot = (to == target).astype(jnp.float32).astype(jnp.bfloat16)

    own_data.wait()
    all_data().wait_recv()
    for c in range(3):
        block = arrived[c]
        if per_peer % 8:
            block = block.astype(jnp.float32).reshape(rows_dev, ncol).astype(jnp.bfloat16)
        else:
            block = block.reshape(rows_dev, ncol)
        stress[c] = lax.dot_general(
            onehot, block, (((0,), (0,)), ((), ())), preferred_element_type=jnp.float32
        )

    pl.loop(0, steps)(geo_first)
    g_sums = lax.fori_loop(0, steps, geo_second, nothing)
    send_sums(0, k_sums + g_sums)
    fill_strip(2, scaled_row(gf))
    third_strips = strip_copies(2, rows_strip)
    for copy in third_strips:
        copy.start()

    read_sums(0)

    @pl.loop(0, steps)
    def _(i):
        s, r0, full, new0, new1 = advanced(i)
        x[0, s, pl.ds(r0 + PAD, chunk), :] = new0
        x[1, s, pl.ds(r0 + PAD, chunk), :] = new1

    @pl.loop(0, steps)
    def _(i):
        stiff_first(i)
        geo_first(i)

    for copy in second_strips + third_strips:
        copy.wait_recv()
    for s in range(slots):
        parts = [[chosen(which, v, s) for v in range(2)] for which in range(3)]
        ends = []
        for end in range(2):
            ends.append(stepped(*(parts[which][v][end] for which in range(3) for v in range(2))))
        for v in range(2):
            set_edge(s, v, ends[0][v], ends[1][v])

    def second(i, acc):
        return stiff_second(i, acc[:3]) + geo_second(i, acc[3:])

    totals = lax.fori_loop(0, steps, second, nothing + nothing)
    send_sums(1, totals)
    read_sums(1)

    @pl.loop(0, steps)
    def _(i):
        s, r0, full, new0, new1 = advanced(i)
        out[0, full, :] = new0
        out[1, full, :] = new1

    for copy in first_strips + second_strips + third_strips:
        copy.wait_send()
    all_ids().wait_send()
    all_data().wait_send()
    all_sums(0).wait_send()
    all_sums(1).wait_send()


def per_device(vectors, prestress, thickness, foundation, patch_rows, matched, elem_row):
    n = lax.axis_size(("patch", "sub", "half"))
    slots = patch_rows.shape[0]
    rows_dev, ncol = thickness.shape
    prows = rows_dev // slots
    per_peer = rows_dev // n
    pre = jnp.transpose(prestress, (1, 0, 2)).reshape(3, n, per_peer, ncol)
    elem = elem_row.reshape(1, rows_dev)
    f32 = jnp.float32
    padded = pltpu.VMEM((2, slots, prows + 2 * PAD, ncol), f32)
    flat = pltpu.VMEM((rows_dev, ncol), f32)
    pair = pltpu.VMEM((2, rows_dev, ncol), f32)
    strip_rows = slots * 8 + -(-slots // 8) * 8
    hbm = pl.BlockSpec(memory_space=pltpu.HBM)
    dma = pltpu.SemaphoreType.DMA
    operands = (vectors, pre, thickness, foundation, patch_rows, matched, elem)
    return pl.pallas_call(
        body,
        out_shape=jax.ShapeDtypeStruct((2, rows_dev, ncol), f32),
        in_specs=[hbm] * 7,
        out_specs=pl.BlockSpec(memory_space=pltpu.VMEM),
        scratch_shapes=[
            pltpu.SMEM((slots,), jnp.int32), pltpu.SMEM((slots,), jnp.int32),
            padded, flat, flat, flat,
            pltpu.VMEM((3, rows_dev, ncol), f32),
            padded, padded, pair, pair, pair, pair,
            pltpu.VMEM((3, n, per_peer, ncol), jnp.bfloat16),
            pltpu.VMEM((n, 1, rows_dev), jnp.int32),
            pltpu.VMEM((3, strip_rows, ncol), f32),
            pltpu.VMEM((3, 2, strip_rows, ncol), f32),
            pltpu.VMEM((slots, 2, 8, ncol), f32),
            pltpu.VMEM((2, n, 1, LANES), f32),
            pltpu.VMEM((8, ncol), f32),
            dma((2 * slots + 2,)), dma((4,)),
            dma((1,)), dma((1,)), dma((1,)), dma((1,)),
            dma((6,)), dma((6,)), dma((2,)), dma((2,)),
        ],
        compiler_params=pltpu.CompilerParams(
            collective_id=0, has_side_effects=True, vmem_limit_bytes=24 << 20
        ),
    )(*(pltpu.with_memory_space_constraint(a, pltpu.HBM) for a in operands))


def solution(mesh):
    split = ("groups", "patch", "sub", "half")
    in_specs = (
        P(None, split, None),
        P(split, None, None),
        P(split, None),
        P(split, None),
        P(split),
        P(split),
        P(split),
    )
    return jax.shard_map(
        per_device, mesh=mesh, in_specs=in_specs, out_specs=P(None, split, None), check_vma=False
    )
```

```python
import jax
import jax.numpy as jnp
from jax import lax
from jax.experimental import pallas as pl
from jax.experimental.pallas import tpu as pltpu
from jax.sharding import PartitionSpec as P

step_size = 1.0
norm_scale = 16.0
penalty_value = 8.0
penalty_slope = 4.0

MESH = pl.DeviceIdType.MESH
PAD = 8
LANES = 128
CHUNK = 128


def body(
    vec, pre, thick_in, found_in, lengths_in, matched_in, elem, out,
    lengths, matched,
    x, thick, found, prec, stress, mrow, frow, kpart, gpart, kf, gf,
    arrived, ids, strips, got, kept, edge, sums, coef,
    load_sem, own_sem, data_send, data_recv, ids_send, ids_recv,
    strip_send, strip_recv, sum_send, sum_recv,
):
    owners, subs, halves = (lax.axis_size(a) for a in ("patch", "sub", "half"))
    n = owners * subs * halves
    pi, si, hi = (lax.axis_index(a) for a in ("patch", "sub", "half"))
    me = (pi * subs + si) * halves + hi
    slots = x.shape[1]
    prows = x.shape[2] - 2 * PAD
    ncol = x.shape[3]
    rows_dev = slots * prows
    per_peer = rows_dev // n
    chunk = CHUNK
    per_slot = prows // chunk
    steps = slots * per_slot

    ends_of = 2 if owners % 2 == 0 else 1
    near = owners // ends_of

    def peer(d):
        step = lax.rem(d + (n // 2 if ends_of == 2 else 0), n)
        side = lax.rem(lax.div(pi, near) + lax.div(step, near * subs * halves), ends_of)
        along = lax.rem(lax.rem(pi, near) + lax.rem(lax.div(step, subs * halves), near), near)
        to_patch = side * near + along
        to_sub = lax.rem(si + lax.rem(lax.div(step, halves), subs), subs)
        to_half = lax.rem(hi + lax.rem(step, halves), halves)
        k = (to_patch * subs + to_sub) * halves + to_half
        return k, {"patch": to_patch, "sub": to_sub, "half": to_half}

    def for_peers(action):
        start = n // 2 if ends_of == 2 else 0

        def one(e):
            d = lax.select(e < start, e, e + 1) if start else e + 1
            action(*peer(d))

        if n <= 16:
            for e in range(n - 1):
                one(jnp.int32(e))
        else:
            pl.loop(0, n - 1)(one)

    barrier = pltpu.get_barrier_semaphore()

    def greet(k, where):
        pl.semaphore_signal(barrier, inc=1, device_id=where, device_id_type=MESH)

    for_peers(greet)

    loads = []
    for v in range(2):
        for s in range(slots):
            loads.append(
                pltpu.make_async_copy(
                    vec.at[v, pl.ds(s * prows, prows)],
                    x.at[v, s, pl.ds(PAD, prows)],
                    load_sem.at[v * slots + s],
                )
            )
    load_thick = pltpu.make_async_copy(thick_in, thick, load_sem.at[2 * slots])
    load_found = pltpu.make_async_copy(found_in, found, load_sem.at[2 * slots + 1])
    own_data = pltpu.make_async_copy(pre.at[:, me], arrived.at[:, me], own_sem.at[0])
    own_ids = pltpu.make_async_copy(elem, ids.at[me], own_sem.at[1])
    load_ints = [
        pltpu.make_async_copy(lengths_in, lengths, own_sem.at[2]),
        pltpu.make_async_copy(matched_in, matched, own_sem.at[3]),
    ]
    for copy in load_ints + loads + [load_thick, load_found, own_data, own_ids]:
        copy.start()

    zero_pad = jnp.zeros((PAD, ncol), jnp.float32)
    for v in range(2):
        for s in range(slots):
            for ref in (x, mrow, frow):
                ref[v, s, 0:PAD, :] = zero_pad
                ref[v, s, PAD + prows : 2 * PAD + prows, :] = zero_pad
    for copy in load_ints + loads:
        copy.wait()

    def fill_strip(which, row_of):
        for s in range(slots):
            length = jnp.maximum(lengths[s], 2)
            for v in range(2):
                base = (s * 2 + v) * 4
                for r, at in enumerate((length - 2, length - 1, 0, 1)):
                    strips[which, base + r : base + r + 1, :] = row_of(s, v, at)

    rows_strip = slots * 2 * 4
    fill_strip(0, lambda s, v, at: x[v, s, pl.ds(PAD + at, 1), :])
    for s in range(slots):
        strips[0, rows_strip + s : rows_strip + s + 1, :] = jnp.full(
            (1, ncol), matched[s], jnp.int32
        ).astype(jnp.float32)

    pl.semaphore_wait(barrier, n - 1)

    def strip_copies(which, rows):
        copies = []
        for side, by in ((0, 1), (1, owners - 1)):
            copies.append(
                pltpu.make_async_remote_copy(
                    src_ref=strips.at[which, pl.ds(0, rows)],
                    dst_ref=got.at[which, side, pl.ds(0, rows)],
                    send_sem=strip_send.at[which * 2 + side],
                    recv_sem=strip_recv.at[which * 2 + side],
                    device_id={"patch": lax.rem(pi + by, owners)},
                    device_id_type=MESH,
                )
            )
        return copies

    first_strips = strip_copies(0, strips.shape[1])
    for copy in first_strips:
        copy.start()

    def send_block(k, where):
        pltpu.make_async_remote_copy(
            src_ref=elem, dst_ref=ids.at[me], send_sem=ids_send.at[0],
            recv_sem=ids_recv.at[0], device_id=where, device_id_type=MESH,
        ).start()
        pltpu.make_async_remote_copy(
            src_ref=pre.at[:, k], dst_ref=arrived.at[:, me], send_sem=data_send.at[0],
            recv_sem=data_recv.at[0], device_id=where, device_id_type=MESH,
        ).start()

    for_peers(send_block)

    def all_ids():
        part = ids.at[pl.ds(0, n - 1)]
        return pltpu.make_async_remote_copy(
            src_ref=part, dst_ref=part, send_sem=ids_send.at[0], recv_sem=ids_recv.at[0],
            device_id={"patch": pi}, device_id_type=MESH,
        )

    def all_data():
        part = arrived.at[:, pl.ds(0, n - 1)]
        return pltpu.make_async_remote_copy(
            src_ref=part, dst_ref=part, send_sem=data_send.at[0], recv_sem=data_recv.at[0],
            device_id={"patch": pi}, device_id_type=MESH,
        )

    lane = lax.broadcasted_iota(jnp.int32, (chunk, ncol), 1)
    first_lane = lane == 0
    last_lane = lane == ncol - 1
    sub_row = lax.broadcasted_iota(jnp.int32, (chunk, ncol), 0)

    def before(w):
        return jnp.where(first_lane, 0.0, pltpu.roll(w, 1, 1))

    def after(w):
        return jnp.where(last_lane, 0.0, pltpu.roll(w, ncol - 1, 1))

    def place(i):
        s = lax.div(i, per_slot)
        r0 = pl.multiple_of(lax.rem(i, per_slot) * chunk, chunk)
        full = pl.multiple_of(i * chunk, chunk)
        return s, r0, pl.ds(full, chunk), r0 + sub_row, lengths[s]

    def shifted(ref, v, s, r0, by):
        window = ref.at[v, s, pl.ds(r0, chunk + 2 * PAD)]
        return window[PAD + by : PAD + by + chunk, :]

    load_thick.wait()
    load_found.wait()

    @pl.loop(0, steps, unroll=True)
    def _(i):
        s, r0, full, row, length = place(i)
        live = row < length
        for v in range(2):
            at = pl.ds(r0 + PAD, chunk)
            x[v, s, at, :] = jnp.where(live, x[v, s, at, :], 0.0)
        prec[full, :] = jnp.where(live, 1.0, 0.0) / (found[full, :] + 12.0 * thick[full, :])

    def stiff_first(i):
        s, r0, full, row, length = place(i)
        th = thick[full, :]
        fo = found[full, :]
        live_th = jnp.where(row < length, th, 0.0)
        for v in range(2):
            w = shifted(x, v, s, r0, 0)
            mrow[v, s, pl.ds(r0 + PAD, chunk), :] = live_th * (
                shifted(x, v, s, r0, -1) - 2.0 * w + shifted(x, v, s, r0, 1)
            )
            bend = th * (before(w) - 2.0 * w + after(w))
            kpart[v, full, :] = fo * w + (before(bend) - 2.0 * bend + after(bend))

    def geo_first(i):
        s, r0, full, row, length = place(i)
        nuu = stress[0, full, :]
        nvv = stress[1, full, :]
        nuv = stress[2, full, :]
        for v in range(2):
            w = shifted(x, v, s, r0, 0)
            along_rows = shifted(x, v, s, r0, 1) - w
            along_cols = after(w) - w
            frow[v, s, pl.ds(r0 + PAD, chunk), :] = nuu * along_rows + nuv * along_cols
            cols = nvv * along_cols + nuv * along_rows
            gpart[v, full, :] = before(cols) - cols

    def fold(value):
        total = value[0:8]
        for j in range(8, chunk, 8):
            total = total + value[j : j + 8]
        return total

    def stiff_second(i, acc):
        s, r0, full, row, length = place(i)
        ks = []
        for v in range(2):
            m = shifted(mrow, v, s, r0, 0)
            bent = shifted(mrow, v, s, r0, -1) - 2.0 * m + shifted(mrow, v, s, r0, 1)
            k = jnp.where(row < length, kpart[v, full, :] + bent, 0.0)

            def line(r):
                return edge[s, v, r : r + 1, :]

            joint = jnp.where(row == length - 1, line(0), 0.0)
            joint = jnp.where(row == length - 2, line(1), joint)
            joint = jnp.where(row == 0, line(2), joint)
            joint = jnp.where(row == 1, line(3), joint)
            k = k + joint
            kf[v, full, :] = k
            ks.append(k)
        x0 = shifted(x, 0, s, r0, 0)
        x1 = shifted(x, 1, s, r0, 0)
        return (
            acc[0] + fold(x0 * ks[0]),
            acc[1] + fold(x0 * ks[1]),
            acc[2] + fold(x1 * ks[1]),
        )

    def geo_second(i, acc):
        s, r0, full, row, length = place(i)
        gs = []
        for v in range(2):
            g = shifted(frow, v, s, r0, -1) - shifted(frow, v, s, r0, 0) + gpart[v, full, :]
            g = jnp.where(row < length, g, 0.0)
            gf[v, full, :] = g
            gs.append(g)
        x0 = shifted(x, 0, s, r0, 0)
        x1 = shifted(x, 1, s, r0, 0)
        return (
            acc[0] + fold(x0 * gs[0]),
            acc[1] + fold(x0 * gs[1]),
            acc[2] + fold(x1 * gs[1]),
        )

    def chosen(which, v, s):
        wanted = jnp.full((2, ncol), matched[s], jnp.int32)
        mine = (me * slots + s).astype(jnp.float32)
        bottom = jnp.zeros((2, ncol), jnp.float32)
        top = jnp.zeros((2, ncol), jnp.float32)
        for side, by in ((0, owners - 1), (1, 1)):
            other = (lax.rem(pi + by, owners) * subs + si) * halves + hi
            for t in range(slots):
                base = (t * 2 + v) * 4
                bottom = bottom + jnp.where(
                    wanted == other * slots + t, got[which, side, base + 2 : base + 4, :], 0.0
                )
                label = got[0, side, rows_strip + t : rows_strip + t + 1, :]
                top = top + jnp.where(label == mine, got[which, side, base : base + 2, :], 0.0)
        return top, bottom

    def keep(which, s, v, top, bottom):
        kept[which, s, v, 0:2, :] = top
        kept[which, s, v, 2:4, :] = bottom

    def set_edge(s, v, partner_top, partner_bottom):
        length = jnp.maximum(lengths[s], 2)
        top0 = x[v, s, pl.ds(PAD + length - 2, 1), :]
        top1 = x[v, s, pl.ds(PAD + length - 1, 1), :]
        bot0 = x[v, s, PAD : PAD + 1, :]
        bot1 = x[v, s, PAD + 1 : PAD + 2, :]
        ptop0, ptop1 = partner_top[0:1], partner_top[1:2]
        pbot0, pbot1 = partner_bottom[0:1], partner_bottom[1:2]
        jump_top = top1 - pbot0
        slope_top = top1 - top0 - (pbot1 - pbot0)
        jump_bottom = ptop1 - bot0
        slope_bottom = ptop1 - ptop0 - (bot1 - bot0)
        edge[s, v, 0:1, :] = penalty_value * jump_top + penalty_slope * slope_top
        edge[s, v, 1:2, :] = -penalty_slope * slope_top
        edge[s, v, 2:3, :] = -penalty_value * jump_bottom + penalty_slope * slope_bottom
        edge[s, v, 3:4, :] = -penalty_slope * slope_bottom

    def sum_copy(it, where):
        return pltpu.make_async_remote_copy(
            src_ref=sums.at[it, me], dst_ref=sums.at[it, me], send_sem=sum_send.at[it],
            recv_sem=sum_recv.at[it], device_id=where, device_id_type=MESH,
        )

    def all_sums(it):
        part = sums.at[it, pl.ds(0, n - 1)]
        return pltpu.make_async_remote_copy(
            src_ref=part, dst_ref=part, send_sem=sum_send.at[it], recv_sem=sum_recv.at[it],
            device_id={"patch": pi}, device_id_type=MESH,
        )

    def put_sums(line, first, totals):
        spot = lax.broadcasted_iota(jnp.int32, (1, LANES), 1)
        for t, total in enumerate(totals, first):
            one = jnp.sum(jnp.sum(total, axis=0, keepdims=True), axis=1, keepdims=True)
            line = jnp.where(spot == t, one, line)
        return line

    def send_sums(it, line):
        sums[it, me] = line

        def send_line(k, where):
            sum_copy(it, where).start()

        for_peers(send_line)

    def read_sums(it):
        all_sums(it).wait_recv()
        line = jnp.sum(sums[it], axis=0)
        first_a, cross_k, second_a, first_g, cross_g, second_g = (
            line[:, t : t + 1] for t in range(6)
        )
        cells = float(n * rows_dev * ncol)
        ratio = cross_k / first_a
        other_a = second_a - ratio * cross_k
        other_q = second_g - 2.0 * ratio * cross_g + ratio * ratio * first_g
        values = (
            ratio,
            first_g / first_a,
            other_q / other_a,
            jnp.sqrt(norm_scale * cells / first_a),
            jnp.sqrt(norm_scale * cells / other_a),
        )
        for t, value in enumerate(values):
            coef[t : t + 1, :] = jnp.broadcast_to(value, (1, ncol))

    def stepped(x0, x1, pk0, pk1, pg0, pg1):
        ratio, mu1, mu2, scale0, scale1 = (coef[t : t + 1, :] for t in range(5))
        new0 = (x0 + step_size * (pg0 - mu1 * pk0)) * scale0
        new1 = (
            (x1 - ratio * x0) + step_size * ((pg1 - ratio * pg0) - mu2 * (pk1 - ratio * pk0))
        ) * scale1
        return new0, new1

    def advanced(i):
        s, r0, full, row, length = place(i)
        ratio, mu1, mu2, scale0, scale1 = (coef[t : t + 1, :] for t in range(5))
        p = step_size * prec[full, :]
        x0 = shifted(x, 0, s, r0, 0)
        k0 = kf[0, full, :]
        g0 = gf[0, full, :]
        new0 = (x0 + p * (g0 - mu1 * k0)) * scale0
        y = shifted(x, 1, s, r0, 0) - ratio * x0
        ky = kf[1, full, :] - ratio * k0
        gy = gf[1, full, :] - ratio * g0
        new1 = (y + p * (gy - mu2 * ky)) * scale1
        return s, r0, full, new0, new1

    nothing = tuple(jnp.zeros((8, ncol), jnp.float32) for _ in range(3))

    pl.loop(0, steps, unroll=True)(stiff_first)
    for copy in first_strips:
        copy.wait_recv()
    for s in range(slots):
        for v in range(2):
            top, bottom = chosen(0, v, s)
            keep(0, s, v, top, bottom)
            set_edge(s, v, top, bottom)
    no_line = jnp.zeros((1, LANES), jnp.float32)
    k_line = put_sums(no_line, 0, lax.fori_loop(0, steps, stiff_second, nothing, unroll=True))

    def scaled_row(ref):
        def pick(s, v, at):
            spot = pl.ds(s * prows + at, 1)
            return prec[spot, :] * ref[v, spot, :]

        return pick

    fill_strip(1, scaled_row(kf))
    second_strips = strip_copies(1, rows_strip)
    for copy in second_strips:
        copy.start()

    own_ids.wait()
    all_ids().wait_recv()
    who = jnp.broadcast_to(ids[...], (n, per_peer, ncol)).reshape(rows_dev, ncol)
    wide_lane = lax.broadcasted_iota(jnp.int32, (rows_dev, ncol), 1)
    wide_row = lax.broadcasted_iota(jnp.int32, (rows_dev, ncol), 0)
    pick = wide_lane == me * per_peer + lax.rem(wide_row, per_peer)
    target = lax.rem(
        jnp.sum(jnp.where(pick, who, 0).astype(jnp.float32), axis=1, keepdims=True).astype(jnp.int32),
        rows_dev,
    )
    to = lax.broadcasted_iota(jnp.int32, (rows_dev, rows_dev), 1)
    onehot = (to == target).astype(jnp.float32).astype(jnp.bfloat16)

    own_data.wait()
    all_data().wait_recv()
    for c in range(3):
        block = arrived[c]
        if per_peer % 8:
            block = block.astype(jnp.float32).reshape(rows_dev, ncol).astype(jnp.bfloat16)
        else:
            block = block.reshape(rows_dev, ncol)
        stress[c] = lax.dot_general(
            onehot, block, (((0,), (0,)), ((), ())), preferred_element_type=jnp.float32
        )

    pl.loop(0, steps, unroll=True)(geo_first)
    g_sums = lax.fori_loop(0, steps, geo_second, nothing, unroll=True)
    send_sums(0, put_sums(k_line, 3, g_sums))
    fill_strip(2, scaled_row(gf))
    third_strips = strip_copies(2, rows_strip)
    for copy in third_strips:
        copy.start()

    for copy in second_strips:
        copy.wait_recv()
    for s in range(slots):
        for v in range(2):
            keep(1, s, v, *chosen(1, v, s))
    read_sums(0)

    @pl.loop(0, steps, unroll=True)
    def _(i):
        s, r0, full, new0, new1 = advanced(i)
        x[0, s, pl.ds(r0 + PAD, chunk), :] = new0
        x[1, s, pl.ds(r0 + PAD, chunk), :] = new1

    @pl.loop(0, steps, unroll=True)
    def _(i):
        stiff_first(i)
        geo_first(i)

    for copy in third_strips:
        copy.wait_recv()
    for s in range(slots):
        last = [jnp.concatenate(chosen(2, v, s), axis=0) for v in range(2)]
        ends = stepped(*(kept[which, s, v, 0:4, :] for which in range(2) for v in range(2)), *last)
        for v in range(2):
            set_edge(s, v, ends[v][0:2], ends[v][2:4])

    def second(i, acc):
        return stiff_second(i, acc[:3]) + geo_second(i, acc[3:])

    totals = lax.fori_loop(0, steps, second, nothing + nothing, unroll=True)
    send_sums(1, put_sums(no_line, 0, totals))
    read_sums(1)

    @pl.loop(0, steps, unroll=True)
    def _(i):
        s, r0, full, new0, new1 = advanced(i)
        out[0, full, :] = new0
        out[1, full, :] = new1

    for copy in first_strips + second_strips + third_strips:
        copy.wait_send()
    all_ids().wait_send()
    all_data().wait_send()
    all_sums(0).wait_send()
    all_sums(1).wait_send()


def per_device(vectors, prestress, thickness, foundation, patch_rows, matched, elem_row):
    n = lax.axis_size(("patch", "sub", "half"))
    slots = patch_rows.shape[0]
    rows_dev, ncol = thickness.shape
    prows = rows_dev // slots
    per_peer = rows_dev // n
    pre = jnp.transpose(prestress, (1, 0, 2)).reshape(3, n, per_peer, ncol)
    elem = elem_row.reshape(1, rows_dev)
    f32 = jnp.float32
    padded = pltpu.VMEM((2, slots, prows + 2 * PAD, ncol), f32)
    flat = pltpu.VMEM((rows_dev, ncol), f32)
    pair = pltpu.VMEM((2, rows_dev, ncol), f32)
    strip_rows = slots * 8 + -(-slots // 8) * 8
    hbm = pl.BlockSpec(memory_space=pltpu.HBM)
    dma = pltpu.SemaphoreType.DMA
    operands = (vectors, pre, thickness, foundation, patch_rows, matched, elem)
    return pl.pallas_call(
        body,
        out_shape=jax.ShapeDtypeStruct((2, rows_dev, ncol), f32),
        in_specs=[hbm] * 7,
        out_specs=pl.BlockSpec(memory_space=pltpu.VMEM),
        scratch_shapes=[
            pltpu.SMEM((slots,), jnp.int32), pltpu.SMEM((slots,), jnp.int32),
            padded, flat, flat, flat,
            pltpu.VMEM((3, rows_dev, ncol), f32),
            padded, padded, pair, pair, pair, pair,
            pltpu.VMEM((3, n, per_peer, ncol), jnp.bfloat16),
            pltpu.VMEM((n, 1, rows_dev), jnp.int32),
            pltpu.VMEM((3, strip_rows, ncol), f32),
            pltpu.VMEM((3, 2, strip_rows, ncol), f32),
            pltpu.VMEM((2, slots, 2, 8, ncol), f32),
            pltpu.VMEM((slots, 2, 8, ncol), f32),
            pltpu.VMEM((2, n, 1, LANES), f32),
            pltpu.VMEM((8, ncol), f32),
            dma((2 * slots + 2,)), dma((4,)),
            dma((1,)), dma((1,)), dma((1,)), dma((1,)),
            dma((6,)), dma((6,)), dma((2,)), dma((2,)),
        ],
        compiler_params=pltpu.CompilerParams(
            collective_id=0, has_side_effects=True, vmem_limit_bytes=24 << 20
        ),
    )(*(pltpu.with_memory_space_constraint(a, pltpu.HBM) for a in operands))


def solution(mesh):
    split = ("groups", "patch", "sub", "half")
    in_specs = (
        P(None, split, None),
        P(split, None, None),
        P(split, None),
        P(split, None),
        P(split),
        P(split),
        P(split),
    )
    return jax.shard_map(
        per_device, mesh=mesh, in_specs=in_specs, out_specs=P(None, split, None), check_vma=False
    )
```

```python
import jax
import jax.numpy as jnp
from jax import lax
from jax.experimental import pallas as pl
from jax.experimental.pallas import tpu as pltpu
from jax.sharding import PartitionSpec as P

step_size = 1.0
norm_scale = 16.0
penalty_value = 8.0
penalty_slope = 4.0

MESH = pl.DeviceIdType.MESH
PAD = 8
LANES = 128
CHUNK = 128


def body(
    vec, pre, thick_in, found_in, lengths_in, matched_in, elem, out,
    lengths, matched,
    x, thick, found, prec, stress, mrow, frow, kpart, gpart, kf, gf,
    arrived, ids, strips, got, kept, edge, sums, coef,
    load_sem, own_sem, data_send, data_recv, ids_send, ids_recv,
    strip_send, strip_recv, sum_send, sum_recv,
):
    owners, subs, halves = (lax.axis_size(a) for a in ("patch", "sub", "half"))
    n = owners * subs * halves
    pi, si, hi = (lax.axis_index(a) for a in ("patch", "sub", "half"))
    me = (pi * subs + si) * halves + hi
    slots = x.shape[1]
    prows = x.shape[2] - 2 * PAD
    ncol = x.shape[3]
    rows_dev = slots * prows
    per_peer = rows_dev // n
    chunk = CHUNK
    per_slot = prows // chunk
    steps = slots * per_slot

    ends_of = 2 if owners % 2 == 0 else 1
    near = owners // ends_of

    def peer(d):
        step = lax.rem(d + (n // 2 if ends_of == 2 else 0), n)
        side = lax.rem(lax.div(pi, near) + lax.div(step, near * subs * halves), ends_of)
        along = lax.rem(lax.rem(pi, near) + lax.rem(lax.div(step, subs * halves), near), near)
        to_patch = side * near + along
        to_sub = lax.rem(si + lax.rem(lax.div(step, halves), subs), subs)
        to_half = lax.rem(hi + lax.rem(step, halves), halves)
        k = (to_patch * subs + to_sub) * halves + to_half
        return k, {"patch": to_patch, "sub": to_sub, "half": to_half}

    def for_peers(action):
        start = n // 2 if ends_of == 2 else 0

        def one(e):
            d = lax.select(e < start, e, e + 1) if start else e + 1
            action(*peer(d))

        if n <= 16:
            for e in range(n - 1):
                one(jnp.int32(e))
        else:
            pl.loop(0, n - 1)(one)

    barrier = pltpu.get_barrier_semaphore()

    def greet(k, where):
        pl.semaphore_signal(barrier, inc=1, device_id=where, device_id_type=MESH)

    for_peers(greet)

    loads = []
    for v in range(2):
        for s in range(slots):
            loads.append(
                pltpu.make_async_copy(
                    vec.at[v, pl.ds(s * prows, prows)],
                    x.at[v, s, pl.ds(PAD, prows)],
                    load_sem.at[v * slots + s],
                )
            )
    load_thick = pltpu.make_async_copy(thick_in, thick, load_sem.at[2 * slots])
    load_found = pltpu.make_async_copy(found_in, found, load_sem.at[2 * slots + 1])
    own_data = pltpu.make_async_copy(pre.at[:, me], arrived.at[:, me], own_sem.at[0])
    own_ids = pltpu.make_async_copy(elem, ids.at[me], own_sem.at[1])
    load_ints = [
        pltpu.make_async_copy(lengths_in, lengths, own_sem.at[2]),
        pltpu.make_async_copy(matched_in, matched, own_sem.at[3]),
    ]
    for copy in load_ints + loads + [load_thick, load_found, own_data, own_ids]:
        copy.start()

    zero_pad = jnp.zeros((PAD, ncol), jnp.float32)
    for v in range(2):
        for s in range(slots):
            for ref in (x, mrow, frow):
                ref[v, s, 0:PAD, :] = zero_pad
                ref[v, s, PAD + prows : 2 * PAD + prows, :] = zero_pad
    for copy in load_ints + loads:
        copy.wait()

    def fill_strip(which, row_of):
        for s in range(slots):
            length = jnp.maximum(lengths[s], 2)
            for v in range(2):
                base = (s * 2 + v) * 4
                for r, at in enumerate((length - 2, length - 1, 0, 1)):
                    strips[which, base + r : base + r + 1, :] = row_of(s, v, at)

    rows_strip = slots * 2 * 4
    fill_strip(0, lambda s, v, at: x[v, s, pl.ds(PAD + at, 1), :])
    for s in range(slots):
        strips[0, rows_strip + s : rows_strip + s + 1, :] = jnp.full(
            (1, ncol), matched[s], jnp.int32
        ).astype(jnp.float32)

    pl.semaphore_wait(barrier, n - 1)

    def strip_copies(which, rows):
        copies = []
        for side, by in ((0, 1), (1, owners - 1)):
            copies.append(
                pltpu.make_async_remote_copy(
                    src_ref=strips.at[which, pl.ds(0, rows)],
                    dst_ref=got.at[which, side, pl.ds(0, rows)],
                    send_sem=strip_send.at[which * 2 + side],
                    recv_sem=strip_recv.at[which * 2 + side],
                    device_id={"patch": lax.rem(pi + by, owners)},
                    device_id_type=MESH,
                )
            )
        return copies

    first_strips = strip_copies(0, strips.shape[1])
    for copy in first_strips:
        copy.start()

    def send_block(k, where):
        pltpu.make_async_remote_copy(
            src_ref=elem, dst_ref=ids.at[me], send_sem=ids_send.at[0],
            recv_sem=ids_recv.at[0], device_id=where, device_id_type=MESH,
        ).start()
        pltpu.make_async_remote_copy(
            src_ref=pre.at[:, k], dst_ref=arrived.at[:, me], send_sem=data_send.at[0],
            recv_sem=data_recv.at[0], device_id=where, device_id_type=MESH,
        ).start()

    for_peers(send_block)

    def all_ids():
        part = ids.at[pl.ds(0, n - 1)]
        return pltpu.make_async_remote_copy(
            src_ref=part, dst_ref=part, send_sem=ids_send.at[0], recv_sem=ids_recv.at[0],
            device_id={"patch": pi}, device_id_type=MESH,
        )

    def all_data():
        part = arrived.at[:, pl.ds(0, n - 1)]
        return pltpu.make_async_remote_copy(
            src_ref=part, dst_ref=part, send_sem=data_send.at[0], recv_sem=data_recv.at[0],
            device_id={"patch": pi}, device_id_type=MESH,
        )

    lane = lax.broadcasted_iota(jnp.int32, (chunk, ncol), 1)
    first_lane = lane == 0
    last_lane = lane == ncol - 1
    sub_row = lax.broadcasted_iota(jnp.int32, (chunk, ncol), 0)

    def before(w):
        return jnp.where(first_lane, 0.0, pltpu.roll(w, 1, 1))

    def after(w):
        return jnp.where(last_lane, 0.0, pltpu.roll(w, ncol - 1, 1))

    def place(i):
        s = lax.div(i, per_slot)
        r0 = pl.multiple_of(lax.rem(i, per_slot) * chunk, chunk)
        full = pl.multiple_of(i * chunk, chunk)
        return s, r0, pl.ds(full, chunk), r0 + sub_row, lengths[s]

    def shifted(ref, v, s, r0, by):
        window = ref.at[v, s, pl.ds(r0, chunk + 2 * PAD)]
        return window[PAD + by : PAD + by + chunk, :]

    load_thick.wait()
    load_found.wait()

    @pl.loop(0, steps, unroll=True)
    def _(i):
        s, r0, full, row, length = place(i)
        live = row < length
        for v in range(2):
            at = pl.ds(r0 + PAD, chunk)
            x[v, s, at, :] = jnp.where(live, x[v, s, at, :], 0.0)
        prec[full, :] = jnp.where(live, 1.0, 0.0) / (found[full, :] + 12.0 * thick[full, :])

    def stiff_first(i):
        s, r0, full, row, length = place(i)
        th = thick[full, :]
        fo = found[full, :]
        live_th = jnp.where(row < length, th, 0.0)
        for v in range(2):
            w = shifted(x, v, s, r0, 0)
            mrow[v, s, pl.ds(r0 + PAD, chunk), :] = live_th * (
                shifted(x, v, s, r0, -1) - 2.0 * w + shifted(x, v, s, r0, 1)
            )
            bend = th * (before(w) - 2.0 * w + after(w))
            kpart[v, full, :] = fo * w + (before(bend) - 2.0 * bend + after(bend))

    def geo_first(i):
        s, r0, full, row, length = place(i)
        nuu = stress[0, full, :]
        nvv = stress[1, full, :]
        nuv = stress[2, full, :]
        for v in range(2):
            w = shifted(x, v, s, r0, 0)
            along_rows = shifted(x, v, s, r0, 1) - w
            along_cols = after(w) - w
            frow[v, s, pl.ds(r0 + PAD, chunk), :] = nuu * along_rows + nuv * along_cols
            cols = nvv * along_cols + nuv * along_rows
            gpart[v, full, :] = before(cols) - cols

    def fold(value):
        total = value[0:8]
        for j in range(8, chunk, 8):
            total = total + value[j : j + 8]
        return total

    def stiff_second(i, acc):
        s, r0, full, row, length = place(i)
        ks = []
        for v in range(2):
            m = shifted(mrow, v, s, r0, 0)
            bent = shifted(mrow, v, s, r0, -1) - 2.0 * m + shifted(mrow, v, s, r0, 1)
            k = jnp.where(row < length, kpart[v, full, :] + bent, 0.0)

            def line(r):
                return edge[s, v, r : r + 1, :]

            joint = jnp.where(row == length - 1, line(0), 0.0)
            joint = jnp.where(row == length - 2, line(1), joint)
            joint = jnp.where(row == 0, line(2), joint)
            joint = jnp.where(row == 1, line(3), joint)
            k = k + joint
            kf[v, full, :] = k
            ks.append(k)
        x0 = shifted(x, 0, s, r0, 0)
        x1 = shifted(x, 1, s, r0, 0)
        return (
            acc[0] + fold(x0 * ks[0]),
            acc[1] + fold(x0 * ks[1]),
            acc[2] + fold(x1 * ks[1]),
        )

    def geo_second(i, acc):
        s, r0, full, row, length = place(i)
        gs = []
        for v in range(2):
            g = shifted(frow, v, s, r0, -1) - shifted(frow, v, s, r0, 0) + gpart[v, full, :]
            g = jnp.where(row < length, g, 0.0)
            gf[v, full, :] = g
            gs.append(g)
        x0 = shifted(x, 0, s, r0, 0)
        x1 = shifted(x, 1, s, r0, 0)
        return (
            acc[0] + fold(x0 * gs[0]),
            acc[1] + fold(x0 * gs[1]),
            acc[2] + fold(x1 * gs[1]),
        )

    def chosen(which, v, s):
        wanted = jnp.full((2, ncol), matched[s], jnp.int32)
        mine = (me * slots + s).astype(jnp.float32)
        bottom = jnp.zeros((2, ncol), jnp.float32)
        top = jnp.zeros((2, ncol), jnp.float32)
        for side, by in ((0, owners - 1), (1, 1)):
            other = (lax.rem(pi + by, owners) * subs + si) * halves + hi
            for t in range(slots):
                base = (t * 2 + v) * 4
                bottom = bottom + jnp.where(
                    wanted == other * slots + t, got[which, side, base + 2 : base + 4, :], 0.0
                )
                label = got[0, side, rows_strip + t : rows_strip + t + 1, :]
                top = top + jnp.where(label == mine, got[which, side, base : base + 2, :], 0.0)
        return top, bottom

    def keep(which, s, v, top, bottom):
        kept[which, s, v, 0:2, :] = top
        kept[which, s, v, 2:4, :] = bottom

    def set_edge(s, v, partner_top, partner_bottom):
        length = jnp.maximum(lengths[s], 2)
        top0 = x[v, s, pl.ds(PAD + length - 2, 1), :]
        top1 = x[v, s, pl.ds(PAD + length - 1, 1), :]
        bot0 = x[v, s, PAD : PAD + 1, :]
        bot1 = x[v, s, PAD + 1 : PAD + 2, :]
        ptop0, ptop1 = partner_top[0:1], partner_top[1:2]
        pbot0, pbot1 = partner_bottom[0:1], partner_bottom[1:2]
        jump_top = top1 - pbot0
        slope_top = top1 - top0 - (pbot1 - pbot0)
        jump_bottom = ptop1 - bot0
        slope_bottom = ptop1 - ptop0 - (bot1 - bot0)
        edge[s, v, 0:1, :] = penalty_value * jump_top + penalty_slope * slope_top
        edge[s, v, 1:2, :] = -penalty_slope * slope_top
        edge[s, v, 2:3, :] = -penalty_value * jump_bottom + penalty_slope * slope_bottom
        edge[s, v, 3:4, :] = -penalty_slope * slope_bottom

    def sum_copy(it, where):
        return pltpu.make_async_remote_copy(
            src_ref=sums.at[it, me], dst_ref=sums.at[it, me], send_sem=sum_send.at[it],
            recv_sem=sum_recv.at[it], device_id=where, device_id_type=MESH,
        )

    def all_sums(it):
        part = sums.at[it, pl.ds(0, n - 1)]
        return pltpu.make_async_remote_copy(
            src_ref=part, dst_ref=part, send_sem=sum_send.at[it], recv_sem=sum_recv.at[it],
            device_id={"patch": pi}, device_id_type=MESH,
        )

    def put_sums(line, first, totals):
        spot = lax.broadcasted_iota(jnp.int32, (1, LANES), 1)
        for t, total in enumerate(totals, first):
            one = jnp.sum(jnp.sum(total, axis=0, keepdims=True), axis=1, keepdims=True)
            line = jnp.where(spot == t, one, line)
        return line

    def send_sums(it, line):
        sums[it, me] = line

        def send_line(k, where):
            sum_copy(it, where).start()

        for_peers(send_line)

    def read_sums(it):
        all_sums(it).wait_recv()
        line = jnp.sum(sums[it], axis=0)
        first_a, cross_k, second_a, first_g, cross_g, second_g = (
            line[:, t : t + 1] for t in range(6)
        )
        cells = float(n * rows_dev * ncol)
        ratio = cross_k / first_a
        other_a = second_a - ratio * cross_k
        other_q = second_g - 2.0 * ratio * cross_g + ratio * ratio * first_g
        values = (
            ratio,
            first_g / first_a,
            other_q / other_a,
            jnp.sqrt(norm_scale * cells / first_a),
            jnp.sqrt(norm_scale * cells / other_a),
        )
        for t, value in enumerate(values):
            coef[t : t + 1, :] = jnp.broadcast_to(value, (1, ncol))

    def stepped(x0, x1, pk0, pk1, pg0, pg1):
        ratio, mu1, mu2, scale0, scale1 = (coef[t : t + 1, :] for t in range(5))
        new0 = (x0 + step_size * (pg0 - mu1 * pk0)) * scale0
        new1 = (
            (x1 - ratio * x0) + step_size * ((pg1 - ratio * pg0) - mu2 * (pk1 - ratio * pk0))
        ) * scale1
        return new0, new1

    def advanced(i):
        s, r0, full, row, length = place(i)
        ratio, mu1, mu2, scale0, scale1 = (coef[t : t + 1, :] for t in range(5))
        p = step_size * prec[full, :]
        x0 = shifted(x, 0, s, r0, 0)
        k0 = kf[0, full, :]
        g0 = gf[0, full, :]
        new0 = (x0 + p * (g0 - mu1 * k0)) * scale0
        y = shifted(x, 1, s, r0, 0) - ratio * x0
        ky = kf[1, full, :] - ratio * k0
        gy = gf[1, full, :] - ratio * g0
        new1 = (y + p * (gy - mu2 * ky)) * scale1
        return s, r0, full, new0, new1

    nothing = tuple(jnp.zeros((8, ncol), jnp.float32) for _ in range(3))

    pl.loop(0, steps, unroll=True)(stiff_first)
    for copy in first_strips:
        copy.wait_recv()
    for s in range(slots):
        for v in range(2):
            top, bottom = chosen(0, v, s)
            keep(0, s, v, top, bottom)
            set_edge(s, v, top, bottom)
    no_line = jnp.zeros((1, LANES), jnp.float32)
    k_line = put_sums(no_line, 0, lax.fori_loop(0, steps, stiff_second, nothing, unroll=True))

    def scaled_row(ref):
        def pick(s, v, at):
            spot = pl.ds(s * prows + at, 1)
            return prec[spot, :] * ref[v, spot, :]

        return pick

    fill_strip(1, scaled_row(kf))
    second_strips = strip_copies(1, rows_strip)

    own_ids.wait()
    all_ids().wait_recv()
    who = jnp.broadcast_to(ids[...], (n, per_peer, ncol)).reshape(rows_dev, ncol)
    wide_lane = lax.broadcasted_iota(jnp.int32, (rows_dev, ncol), 1)
    wide_row = lax.broadcasted_iota(jnp.int32, (rows_dev, ncol), 0)
    pick = wide_lane == me * per_peer + lax.rem(wide_row, per_peer)
    target = lax.rem(
        jnp.sum(jnp.where(pick, who, 0).astype(jnp.float32), axis=1, keepdims=True).astype(jnp.int32),
        rows_dev,
    )
    to = lax.broadcasted_iota(jnp.int32, (rows_dev, rows_dev), 1)
    onehot = (to == target).astype(jnp.float32).astype(jnp.bfloat16)

    own_data.wait()
    all_data().wait_recv()
    for copy in second_strips:
        copy.start()
    for c in range(3):
        block = arrived[c]
        if per_peer % 8:
            block = block.astype(jnp.float32).reshape(rows_dev, ncol).astype(jnp.bfloat16)
        else:
            block = block.reshape(rows_dev, ncol)
        stress[c] = lax.dot_general(
            onehot, block, (((0,), (0,)), ((), ())), preferred_element_type=jnp.float32
        )

    pl.loop(0, steps, unroll=True)(geo_first)
    g_sums = lax.fori_loop(0, steps, geo_second, nothing, unroll=True)
    send_sums(0, put_sums(k_line, 3, g_sums))
    fill_strip(2, scaled_row(gf))
    third_strips = strip_copies(2, rows_strip)
    for copy in third_strips:
        copy.start()

    for copy in second_strips:
        copy.wait_recv()
    for s in range(slots):
        for v in range(2):
            keep(1, s, v, *chosen(1, v, s))
    read_sums(0)

    @pl.loop(0, steps, unroll=True)
    def _(i):
        s, r0, full, new0, new1 = advanced(i)
        x[0, s, pl.ds(r0 + PAD, chunk), :] = new0
        x[1, s, pl.ds(r0 + PAD, chunk), :] = new1

    @pl.loop(0, steps, unroll=True)
    def _(i):
        stiff_first(i)
        geo_first(i)

    for copy in third_strips:
        copy.wait_recv()
    for s in range(slots):
        last = [jnp.concatenate(chosen(2, v, s), axis=0) for v in range(2)]
        ends = stepped(*(kept[which, s, v, 0:4, :] for which in range(2) for v in range(2)), *last)
        for v in range(2):
            set_edge(s, v, ends[v][0:2], ends[v][2:4])

    def second(i, acc):
        return stiff_second(i, acc[:3]) + geo_second(i, acc[3:])

    totals = lax.fori_loop(0, steps, second, nothing + nothing, unroll=True)
    send_sums(1, put_sums(no_line, 0, totals))
    read_sums(1)

    @pl.loop(0, steps, unroll=True)
    def _(i):
        s, r0, full, new0, new1 = advanced(i)
        out[0, full, :] = new0
        out[1, full, :] = new1

    for copy in first_strips + second_strips + third_strips:
        copy.wait_send()
    all_ids().wait_send()
    all_data().wait_send()
    all_sums(0).wait_send()
    all_sums(1).wait_send()


def per_device(vectors, prestress, thickness, foundation, patch_rows, matched, elem_row):
    n = lax.axis_size(("patch", "sub", "half"))
    slots = patch_rows.shape[0]
    rows_dev, ncol = thickness.shape
    prows = rows_dev // slots
    per_peer = rows_dev // n
    pre = jnp.transpose(prestress, (1, 0, 2)).reshape(3, n, per_peer, ncol)
    elem = elem_row.reshape(1, rows_dev)
    f32 = jnp.float32
    padded = pltpu.VMEM((2, slots, prows + 2 * PAD, ncol), f32)
    flat = pltpu.VMEM((rows_dev, ncol), f32)
    pair = pltpu.VMEM((2, rows_dev, ncol), f32)
    strip_rows = slots * 8 + -(-slots // 8) * 8
    hbm = pl.BlockSpec(memory_space=pltpu.HBM)
    dma = pltpu.SemaphoreType.DMA
    operands = (vectors, pre, thickness, foundation, patch_rows, matched, elem)
    return pl.pallas_call(
        body,
        out_shape=jax.ShapeDtypeStruct((2, rows_dev, ncol), f32),
        in_specs=[hbm] * 7,
        out_specs=pl.BlockSpec(memory_space=pltpu.VMEM),
        scratch_shapes=[
            pltpu.SMEM((slots,), jnp.int32), pltpu.SMEM((slots,), jnp.int32),
            padded, flat, flat, flat,
            pltpu.VMEM((3, rows_dev, ncol), f32),
            padded, padded, pair, pair, pair, pair,
            pltpu.VMEM((3, n, per_peer, ncol), jnp.bfloat16),
            pltpu.VMEM((n, 1, rows_dev), jnp.int32),
            pltpu.VMEM((3, strip_rows, ncol), f32),
            pltpu.VMEM((3, 2, strip_rows, ncol), f32),
            pltpu.VMEM((2, slots, 2, 8, ncol), f32),
            pltpu.VMEM((slots, 2, 8, ncol), f32),
            pltpu.VMEM((2, n, 1, LANES), f32),
            pltpu.VMEM((8, ncol), f32),
            dma((2 * slots + 2,)), dma((4,)),
            dma((1,)), dma((1,)), dma((1,)), dma((1,)),
            dma((6,)), dma((6,)), dma((2,)), dma((2,)),
        ],
        compiler_params=pltpu.CompilerParams(
            collective_id=0, has_side_effects=True, vmem_limit_bytes=24 << 20
        ),
    )(*(pltpu.with_memory_space_constraint(a, pltpu.HBM) for a in operands))


def solution(mesh):
    split = ("groups", "patch", "sub", "half")
    in_specs = (
        P(None, split, None),
        P(split, None, None),
        P(split, None),
        P(split, None),
        P(split),
        P(split),
        P(split),
    )
    return jax.shard_map(
        per_device, mesh=mesh, in_specs=in_specs, out_specs=P(None, split, None), check_vma=False
    )
```
